256 devices in a mesh: section: 64 (over y_hi, x, z), dp: 4 (over y_lo, core).
Axes of the slice: x: 4, y: 4 (y_hi: 2, y_lo: 2; y = y_hi * 2 + y_lo), z: 8, core: 2. Of those that a mesh axis runs over, the one named last changes fastest.
Arguments:
- streams: bfloat16 [2, 64, 4, 128, 1024], P(None, 'section', 'dp'), may hold values from -45 to 45
- cotangents: bfloat16 [2, 64, 4, 128, 1024], P(None, 'section', 'dp'), may hold values from -6 to 6
- weights: bfloat16 [64, 1024, 4096], P('section'), may hold values from -0.1875 to 0.1875
- norm_gains: float32 [64, 1024], P('section'), may hold values from 0.25 to 1.75
- segment_ids: int32 [64, 4, 128], P(None, 'dp'), may hold values from 0 to 1, never falling along the last dimension, each value on 1 to 96 neighbouring positions
Outputs:
- out_streams: bfloat16 [2, 64, 4, 128, 1024], P(None, 'section', 'dp')
- out_cotangents: bfloat16 [2, 64, 4, 128, 1024], P(None, 'section', 'dp')
- weight_grads: bfloat16 [64, 1024, 4096], P('section', 'dp')
- gain_grads: float32 [64, 1024], P('section', 'dp')
The draws below stay inside these ranges and needn't reach their ends.
Inputs may be any that keep to these rules, and one draw needn't show every extreme that they name: `segment_ids`: along each row of 128 tokens the document numbers never fall; each row is a 128-token window of packed documents, attention stays inside the window, and each document has 1 to 96 tokens in it.
All inputs are finite; a program needn't handle non-finite values.
Results may differ from the reference program's by a relative error of at most 0.018.
Values may be sent and summed in bfloat16 or wider, within the bound.
No kernel may reach another device: no remote copies, remote signals or barrier semaphores. Data moves between devices by JAX's collectives and lax.ppermute only.
A program may use at most 128 MiB of HBM per device.

```python
import math
import jax
import jax.numpy as jnp
import numpy as np
from jax import lax

D = 1024
HEADS = 16
FF = 2048
ROWS = 128
TICKS = 3
SEG_COUNT = 2
SEG_MOST = 96
SECTIONS = 64
REPLICAS = 4
TOKENS_SUMMED = 1536


def draw_streams(key, part):
    subkeys = jax.random.split(key, 3)
    full_shape = (2, SECTIONS, REPLICAS, ROWS, D)
    log_low = math.log(0.3)
    log_high = math.log(3.0)
    row_scale = jnp.exp(jax.random.uniform(subkeys[0], (2, SECTIONS, REPLICAS, ROWS, 1), jnp.float32, log_low, log_high))
    col_scale = jnp.exp(jax.random.uniform(subkeys[1], (2, SECTIONS, REPLICAS, 1, D), jnp.float32, log_low, log_high))
    base_values = jax.random.normal(subkeys[2], full_shape, jnp.float32)
    base_values = jnp.clip(base_values, -5.0, 5.0)
    return (base_values * row_scale * col_scale).astype(jnp.bfloat16)


def block_levels(rng, extent, cuts, least, high):
    def one(dim, shards_of):
        steps = jax.random.uniform(jax.random.fold_in(jax.random.fold_in(rng, 6), dim), (shards_of,), jnp.float32, least / len(cuts), high / len(cuts))
        return jnp.repeat(jnp.exp(steps), extent[dim] // shards_of).reshape((-1,) + (1,) * (len(extent) - dim - 1))

    level = one(*cuts[0])
    for cut in cuts[1:]:
        level = level * one(*cut)
    return level


def profile(number_of, total, most, slope):
    portions = [(1 << 20) // math.isqrt(rank ** slope) + 1 for rank in range(2, number_of + 1)]
    surplus, counts = total - most - (number_of - 1), [1] * (number_of - 1)
    while surplus > 0:
        movable = [i for i in range(number_of - 1) if counts[i] < most]
        mass, remaining = sum([portions[i] for i in movable]), surplus
        for i in movable:
            extra = min(most - counts[i], max(1, remaining * portions[i] // mass), surplus)
            counts[i] = counts[i] + extra
            surplus = surplus - extra
    return np.array([most] + counts)


def ragged(key, amount, total, limit, lean):
    if amount == 2:
        one = jax.random.randint(key, (), max(1, total - limit), min(limit, total - 1) + 1)
        return jnp.stack([one, total - one])
    sizes = jnp.asarray(profile(amount, total, limit, lean), jnp.int32)
    couples = (amount - 1) // 2
    giver, taker = sizes[1:1 + 2 * couples:2], sizes[2:2 + 2 * couples:2]
    room = jnp.minimum(giver - 1, limit - taker)
    passed = jax.random.randint(jax.random.fold_in(key, 1), (couples,), 0, 1 << 20) % (room + 1)
    sizes = sizes.at[1:1 + 2 * couples:2].set(giver - passed).at[2:2 + 2 * couples:2].set(taker + passed)
    return sizes[jax.random.permutation(jax.random.fold_in(key, 2), amount)]


def noise(stream_key, extent, scale, reach, cuts=(), held_as=jnp.bfloat16):
    loudness = block_levels(stream_key, extent, cuts, -0.22, 0.18) if cuts else 1.0
    entries = jax.random.normal(stream_key, extent, jnp.float32) * scale * loudness
    return jnp.minimum(jnp.maximum(entries, -reach), reach).astype(held_as)


def setup_inputs(seed: int = 0) -> dict:
    keys = jax.random.split(jax.random.key(seed), 6)
    return {
        "streams": draw_streams(jax.random.fold_in(keys[5], 71), 0),
        "cotangents": noise(keys[1], (2, SECTIONS, REPLICAS, ROWS, D), 1.0, 6.0, ((1, 64), (2, 4))),
        "weights": noise(keys[2], (SECTIONS, D, 4 * D), D ** -0.5, 0.1875, ((0, 64),)),
        "norm_gains": jnp.clip(1.0 + 0.15 * jax.random.normal(keys[3], (SECTIONS, D), jnp.float32), 0.25, 1.75),
        "segment_ids": jax.vmap(lambda own: jnp.searchsorted(jnp.cumsum(ragged(own, SEG_COUNT, ROWS, SEG_MOST, 2)), jnp.arange(ROWS), side="right"))(jax.random.split(keys[4], SECTIONS * REPLICAS)).reshape((SECTIONS, REPLICAS, ROWS)).astype(jnp.int32),
    }


epsilon = 1e-05
contract_rows = (((0,), (0,)), ((), ()))
contract_cols = (((1,), (1,)), ((), ()))

def rounded(values):
    return lax.optimization_barrier(values.astype(jnp.bfloat16)).astype(jnp.float32)

def normalize(stream, gain_row):
    mean_square = lax.optimization_barrier(jnp.mean(stream * stream, axis=-1, keepdims=True))
    return stream * lax.rsqrt(mean_square + epsilon) * gain_row

def head_norm(values):
    mean_square = lax.optimization_barrier(jnp.mean(values * values, axis=-1, keepdims=True))
    return values * lax.rsqrt(mean_square + epsilon)

def attend(projected, segment_row):
    row_count = projected.shape[0]
    head_size = D // HEADS
    split_heads = projected.reshape(row_count, 3, HEADS, head_size)
    queries = rounded(head_norm(split_heads[:, 0]))
    key_part = rounded(head_norm(split_heads[:, 1]))
    value_part = rounded(split_heads[:, 2])
    scores = jnp.einsum('qhd,khd->hqk', queries, key_part) / math.sqrt(head_size)
    positions = jnp.arange(row_count)
    allowed = (segment_row[:, None] == segment_row[None, :]) & (positions[None, :] <= positions[:, None])
    raised = jnp.where(allowed[None], jnp.exp(scores), 0.0)
    soft_weights = rounded(raised / lax.optimization_barrier(jnp.sum(raised, axis=-1, keepdims=True)))
    mixture = jnp.einsum('hqk,khd->qhd', soft_weights, value_part)
    return mixture.reshape(row_count, D)

def times_transposed(first, second):
    return lax.dot_general(first, second, contract_cols, preferred_element_type=jnp.float32)

def attention_block(state_now, gain_row, weight, segment_row):
    upper_stream, lower_stream, cot_upper, cot_lower = state_now
    stream = upper_stream.astype(jnp.float32)
    normed = normalize(stream, gain_row).astype(jnp.bfloat16)
    projected = jnp.dot(normed, weight[:, :3 * D], preferred_element_type=jnp.float32)
    mixture, core_back = jax.vjp(lambda inner: attend(inner, segment_row), projected)
    mixture = mixture.astype(jnp.bfloat16)
    branch = jnp.dot(mixture, weight[:, 3 * D:], preferred_element_type=jnp.float32)
    restored = (lower_stream.astype(jnp.float32) - branch).astype(jnp.bfloat16)
    grad_mixture = times_transposed(cot_lower, weight[:, 3 * D:])
    grad_projected = core_back(grad_mixture)[0].astype(jnp.bfloat16)
    grad_normed = times_transposed(grad_projected, weight[:, :3 * D])
    grad_stream, grad_gain = jax.vjp(normalize, stream, gain_row)[1](grad_normed)
    cot_new = (cot_upper.astype(jnp.float32) + grad_stream).astype(jnp.bfloat16)
    new_state = (restored, upper_stream, cot_lower, cot_new)
    left_rows = jnp.concatenate([normed, mixture], axis=1)
    right_rows = jnp.concatenate([grad_projected, cot_lower], axis=1)
    return (new_state, left_rows, right_rows, grad_gain)

def mlp_block(state_now, gain_row, weight, segment_row):
    upper_stream, lower_stream, cot_upper, cot_lower = state_now
    stream = upper_stream.astype(jnp.float32)
    normed = normalize(stream, gain_row).astype(jnp.bfloat16)
    before_act = jnp.dot(normed, weight[:, :FF], preferred_element_type=jnp.float32)
    hidden, gelu_back = jax.vjp(jax.nn.gelu, before_act)
    hidden = hidden.astype(jnp.bfloat16)
    branch = times_transposed(hidden, weight[:, FF:])
    restored = (lower_stream.astype(jnp.float32) - branch).astype(jnp.bfloat16)
    grad_hidden = jnp.dot(cot_lower, weight[:, FF:], preferred_element_type=jnp.float32)
    grad_before = gelu_back(grad_hidden)[0].astype(jnp.bfloat16)
    grad_normed = times_transposed(grad_before, weight[:, :FF])
    grad_stream, grad_gain = jax.vjp(normalize, stream, gain_row)[1](grad_normed)
    cot_new = (cot_upper.astype(jnp.float32) + grad_stream).astype(jnp.bfloat16)
    new_state = (restored, upper_stream, cot_lower, cot_new)
    left_rows = jnp.concatenate([normed, cot_lower], axis=1)
    right_rows = jnp.concatenate([grad_before, hidden], axis=1)
    return (new_state, left_rows, right_rows, grad_gain)

def weight_grad(left_first, left_second, right_rows, split):
    first = lax.dot_general(left_first, right_rows[:, :split], contract_rows, preferred_element_type=jnp.float32)
    second = lax.dot_general(left_second, right_rows[:, split:], contract_rows, preferred_element_type=jnp.float32)
    return jnp.concatenate([first, second], axis=1)

def section_pair(items):
    state_pair, weight_pair, gain_pair, segment_pair = items
    outputs = []
    for kind_index, block_fn in enumerate((attention_block, mlp_block)):

        def replica_step(replica_items, block_fn=block_fn, kind_index=kind_index):
            state_now, segment_row = replica_items
            return block_fn(state_now, gain_pair[kind_index], weight_pair[kind_index], segment_row)
        members = tuple((member[kind_index] for member in state_pair))
        outputs.append(lax.map(replica_step, (members, segment_pair[kind_index])))
    return jax.tree.map(lambda first, second: jnp.stack([first, second]), outputs[0], outputs[1])

def reference(streams, cotangents, weights, norm_gains, segment_ids):
    pair_count = SECTIONS // 2

    def paired(array):
        return array.reshape((pair_count, 2) + array.shape[1:])

    def unpaired(array):
        return array.reshape((SECTIONS,) + array.shape[2:])
    state_now = (streams[0], streams[1], cotangents[0], cotangents[1])
    left_ticks, right_ticks = ([], [])
    gain_total = jnp.zeros((SECTIONS, REPLICAS, D), jnp.float32)
    for tick_index in range(TICKS):
        segments_now = jnp.roll(segment_ids, -tick_index, axis=0)
        result = lax.map(section_pair, (tuple((paired(member) for member in state_now)), paired(weights), paired(norm_gains), paired(segments_now)))
        new_state, left_rows, right_rows, grad_gain = jax.tree.map(unpaired, result)
        left_ticks.append(left_rows)
        right_ticks.append(right_rows)
        gain_total = gain_total + grad_gain
        state_now = tuple((jnp.roll(member, -1, axis=0) for member in new_state))
    left_all = jnp.concatenate(left_ticks, axis=2)
    right_all = jnp.concatenate(right_ticks, axis=2)
    grad_scale = 1.0 / math.sqrt(TOKENS_SUMMED)

    def section_grads(items):
        left_pair, right_pair = items
        grads = []
        for kind_index, split in enumerate((3 * D, FF)):

            def replica_grad(replica_items, split=split):
                left_rows, right_rows = replica_items
                return rounded(weight_grad(left_rows[:, :D], left_rows[:, D:], right_rows, split))
            summed = lax.optimization_barrier(jnp.sum(lax.map(replica_grad, (left_pair[kind_index], right_pair[kind_index])), axis=0))
            grads.append((summed * grad_scale).astype(jnp.bfloat16))
        return jnp.stack(grads)
    weight_grads = unpaired(lax.map(section_grads, (paired(left_all), paired(right_all))))
    gain_grads = lax.optimization_barrier(jnp.sum(rounded(gain_total), axis=1)) * grad_scale
    out_streams = jnp.stack([state_now[0], state_now[1]])
    out_cotangents = jnp.stack([state_now[2], state_now[3]])
    return (out_streams, out_cotangents, weight_grads, gain_grads)
```

```python
import math

import jax
import jax.numpy as jnp
from jax import lax
from jax.experimental import pallas as pl
from jax.experimental.pallas import tpu as pltpu
from jax.sharding import PartitionSpec as P


D = 1024
FF = 2048
TICKS = 3
CHUNK = 512
CHUNKS = 4 * D // CHUNK
PAIR = 128
QUARTER = D // 4

epsilon = 1e-05
bf16 = jnp.bfloat16
f32 = jnp.float32

NN = (((1,), (0,)), ((), ()))
NT = (((1,), (1,)), ((), ()))
TN = (((0,), (0,)), ((), ()))


def dot(first, second, dims=NN):
    return lax.dot_general(first, second, dims, preferred_element_type=f32)


def cols(index, width):
    return pl.ds(index * width, width)


def weight_copies(w_hbm, w_ref, sems, order):
    copies = {}
    for chunk in order:
        piece = cols(chunk, CHUNK)
        copies[chunk] = pltpu.make_async_copy(
            w_hbm.at[:, piece], w_ref.at[:, piece], sems.at[chunk]
        )
    for chunk in order:
        copies[chunk].start()
    return copies


def low_lanes(rows):
    return lax.broadcasted_iota(jnp.int32, (rows, PAIR), 1) < 64


def half_sums(values, low):
    first = jnp.sum(jnp.where(low, values, 0.0), axis=-1, keepdims=True)
    second = jnp.sum(jnp.where(low, 0.0, values), axis=-1, keepdims=True)
    return first, second


def attention_mask(info_ref, seg_ref):
    rows = seg_ref.shape[1]
    segment = seg_ref[pl.ds(info_ref[1], 1), :].astype(f32)
    across = jnp.broadcast_to(segment, (rows, rows))
    down = across.T
    row_index = lax.broadcasted_iota(jnp.int32, (rows, rows), 0)
    col_index = lax.broadcasted_iota(jnp.int32, (rows, rows), 1)
    allowed = (across == down) & (col_index <= row_index)
    mask = jnp.where(allowed, 1.0, 0.0)
    return jnp.concatenate([mask, mask], axis=0)


def split_pair(values, low_b, high_b):
    return jnp.concatenate([values * low_b, values * high_b], axis=0)


def pair_weights(q_ref, k_ref, lane, mask, low_b, high_b):
    q_split = split_pair(q_ref[:, lane], low_b, high_b)
    k = k_ref[:, lane]
    scores = dot(q_split, k, NT) * 0.125
    raised = jnp.exp(scores) * mask
    total = jnp.sum(raised, axis=-1, keepdims=True)
    return q_split, k, raised / total


GELU_A = math.sqrt(2.0 / math.pi)
GELU_B = 0.044715


def forward_kernel(info_ref, y1_ref, y2_ref, g_ref, seg_ref, w_hbm,
                   a_ref, n_ref, x2_ref, s1_ref, s2_ref, w_ref, acc_ref, sems):
    copies = weight_copies(w_hbm, w_ref, sems, range(CHUNKS))
    rows = y1_ref.shape[0]
    stream = y1_ref[...].astype(f32)
    mean_square = jnp.mean(stream * stream, axis=-1, keepdims=True)
    n_ref[...] = (stream * lax.rsqrt(mean_square + epsilon) * g_ref[...]).astype(bf16)

    @pl.when(info_ref[0] == 0)
    def _():
        low = low_lanes(rows)
        low_b = jnp.where(low, 1.0, 0.0).astype(bf16)
        high_b = jnp.where(low, 0.0, 1.0).astype(bf16)
        lane_index = lax.broadcasted_iota(jnp.int32, (rows, PAIR), 1)
        scales = jnp.zeros((rows, PAIR), f32)
        for chunk in range(6):
            copies[chunk].wait()
            projected = dot(n_ref[...], w_ref[:, cols(chunk, CHUNK)])
            for inner in range(CHUNK // PAIR):
                part = projected[:, inner * PAIR:(inner + 1) * PAIR]
                pair = chunk * (CHUNK // PAIR) + inner
                if chunk < 4:
                    first, second = half_sums(part * part, low)
                    r_first = lax.rsqrt(first * (1.0 / 64) + epsilon)
                    r_second = lax.rsqrt(second * (1.0 / 64) + epsilon)
                    scales = jnp.where(lane_index == 2 * pair, r_first, scales)
                    scales = jnp.where(lane_index == 2 * pair + 1, r_second, scales)
                    part = part * jnp.where(low, r_first, r_second)
                s2_ref[:, cols(pair, PAIR)] = part.astype(bf16)
        s1_ref[:, :PAIR] = scales
        mask = attention_mask(info_ref, seg_ref)
        for pair in range(8):
            _, _, weights = pair_weights(
                s2_ref.at[:, :D], s2_ref.at[:, D:2 * D], cols(pair, PAIR), mask, low_b, high_b
            )
            soft = weights.astype(bf16)
            v = s2_ref[:, cols(16 + pair, PAIR)]
            mixed = dot(soft[:rows], v * low_b) + dot(soft[rows:], v * high_b)
            x2_ref[:, cols(pair, PAIR)] = mixed.astype(bf16)
        for chunk in (6, 7):
            copies[chunk].wait()
            out = cols(chunk - 6, CHUNK)
            branch = dot(x2_ref[:, :D], w_ref[:, cols(chunk, CHUNK)])
            a_ref[:, out] = (y2_ref[:, out].astype(f32) - branch).astype(bf16)

    @pl.when(info_ref[0] == 1)
    def _():
        for chunk in range(4):
            copies[chunk].wait()
            piece = cols(chunk, CHUNK)
            pre = dot(n_ref[...], w_ref[:, piece])
            square = pre * pre
            bend = jnp.tanh(GELU_A * (pre + GELU_B * (pre * square)))
            half = 0.5 * (1.0 + bend)
            x2_ref[:, piece] = (pre * half).astype(bf16)
            slope = GELU_A * (1.0 + (3.0 * GELU_B) * square)
            s1_ref[:, piece] = half + 0.5 * pre * (1.0 - bend * bend) * slope
        for chunk in range(4, 8):
            copies[chunk].wait()
            term = dot(x2_ref[:, cols(chunk - 4, CHUNK)], w_ref[:, cols(chunk, CHUNK)], NT)
            if chunk == 4:
                acc_ref[...] = term
            else:
                acc_ref[...] += term
        a_ref[...] = (y2_ref[...].astype(f32) - acc_ref[...]).astype(bf16)


def backward_kernel(info_ref, y1_ref, c1_ref, c2_ref, g_ref, seg_ref, dg_in_ref,
                    n_ref, x2_ref, s1_ref, s2_ref, w_hbm,
                    c_ref, right_ref, keep_ref, send_ref, dg_ref, w_ref, acc_ref, sems):
    copies = weight_copies(w_hbm, w_ref, sems, (6, 7, 4, 5, 0, 1, 2, 3))
    rows = y1_ref.shape[0]
    chip, core = info_ref[2], info_ref[3]
    blocks = (2 * chip + core, 2 * (1 - chip) + core)
    other = (2 * chip + 1 - core, 2 * (1 - chip) + 1 - core)

    def spread(left, half):
        for place, (mine, theirs) in enumerate(zip(blocks, other)):
            out = cols(2 * half + place, QUARTER)
            keep_ref[:, out] = left[:, pl.ds(pl.multiple_of(mine * QUARTER, QUARTER), QUARTER)]
            send_ref[:, out] = left[:, pl.ds(pl.multiple_of(theirs * QUARTER, QUARTER), QUARTER)]

    spread(n_ref, 0)

    @pl.when(info_ref[0] == 0)
    def _():
        spread(x2_ref, 1)
        right_ref[:, 3 * D:] = c2_ref[...]
        low = low_lanes(rows)
        low_b = jnp.where(low, 1.0, 0.0).astype(bf16)
        high_b = jnp.where(low, 0.0, 1.0).astype(bf16)
        mask = attention_mask(info_ref, seg_ref)
        for chunk in (6, 7):
            copies[chunk].wait()
            term = dot(c2_ref[:, cols(chunk - 6, CHUNK)], w_ref[:, cols(chunk, CHUNK)], NT)
            if chunk == 6:
                acc_ref[...] = term
            else:
                acc_ref[...] += term

        def norm_back(dy, y_b, pair):
            dy = dy.astype(bf16).astype(f32)
            y = y_b.astype(f32)
            first, second = half_sums(dy * y, low)
            mean = jnp.where(low, first, second) * (1.0 / 64)
            scale = jnp.where(low, s1_ref[:, 2 * pair:2 * pair + 1], s1_ref[:, 2 * pair + 1:2 * pair + 2])
            return (scale * (dy - y * mean)).astype(bf16)

        for pair in range(8):
            lane = cols(pair, PAIR)
            q_split, k, weights = pair_weights(
                s2_ref.at[:, :D], s2_ref.at[:, D:2 * D], lane, mask, low_b, high_b
            )
            soft = weights.astype(bf16)
            v = s2_ref[:, cols(16 + pair, PAIR)]
            d_mix = split_pair(acc_ref[:, lane].astype(bf16), low_b, high_b)
            d_soft = dot(d_mix, v, NT).astype(bf16).astype(f32)
            dv = dot(soft, d_mix, TN)
            product = d_soft * weights
            d_scores = (product - weights * jnp.sum(product, axis=-1, keepdims=True)) * 0.125
            d_scores = d_scores.astype(bf16)
            dq = dot(d_scores[:rows], k * low_b) + dot(d_scores[rows:], k * high_b)
            dk = dot(d_scores, q_split, TN)
            right_ref[:, lane] = norm_back(dq, s2_ref[:, lane], pair)
            right_ref[:, cols(8 + pair, PAIR)] = norm_back(dk, k, 8 + pair)
            right_ref[:, cols(16 + pair, PAIR)] = dv.astype(bf16)
        for chunk in (4, 5, 0, 1, 2, 3):
            copies[chunk].wait()
            term = dot(right_ref[:, cols(chunk, CHUNK)], w_ref[:, cols(chunk, CHUNK)], NT)
            if chunk == 4:
                acc_ref[...] = term
            else:
                acc_ref[...] += term

    @pl.when(info_ref[0] == 1)
    def _():
        spread(c2_ref, 1)
        right_ref[:, FF:] = x2_ref[...]
        for chunk in (6, 7, 4, 5):
            copies[chunk].wait()
            piece = cols(chunk - 4, CHUNK)
            grad = dot(c2_ref[...], w_ref[:, cols(chunk, CHUNK)])
            right_ref[:, piece] = (grad * s1_ref[:, piece]).astype(bf16)
        for chunk in range(4):
            copies[chunk].wait()
            term = dot(right_ref[:, cols(chunk, CHUNK)], w_ref[:, cols(chunk, CHUNK)], NT)
            if chunk == 0:
                acc_ref[...] = term
            else:
                acc_ref[...] += term

    stream = y1_ref[...].astype(f32)
    inverse = lax.rsqrt(jnp.mean(stream * stream, axis=-1, keepdims=True) + epsilon)
    unit = stream * inverse
    grad_normed = acc_ref[...]
    dg_ref[...] = dg_in_ref[...] + jnp.sum(grad_normed * unit, axis=0, keepdims=True)
    scaled = grad_normed * g_ref[...]
    du = inverse * (scaled - unit * jnp.mean(scaled * unit, axis=-1, keepdims=True))
    c_ref[...] = (c1_ref[...].astype(f32) + du).astype(bf16)


def vmem():
    return pl.BlockSpec(memory_space=pltpu.VMEM)


def smem():
    return pl.BlockSpec(memory_space=pltpu.SMEM)


def anyspace():
    return pl.BlockSpec(memory_space=pl.ANY)


def shape(dims, dtype=bf16):
    return jax.ShapeDtypeStruct(dims, dtype)


MIB = 1 << 20


def forward(info, y1, y2, gain, segments, weight):
    rows = y1.shape[0]
    return pl.pallas_call(
        forward_kernel,
        out_shape=(
            shape((rows, D)), shape((rows, D)), shape((rows, FF)),
            shape((rows, FF), f32), shape((rows, 3 * D)),
        ),
        in_specs=[smem(), vmem(), vmem(), vmem(), vmem(), anyspace()],
        out_specs=(vmem(),) * 5,
        scratch_shapes=[
            pltpu.VMEM((D, 4 * D), bf16), pltpu.VMEM((rows, D), f32),
            pltpu.SemaphoreType.DMA((CHUNKS,)),
        ],
        cost_estimate=pl.CostEstimate(
            flops=8 * rows * D * D, bytes_accessed=12 * MIB, transcendentals=rows * FF
        ),
        name="tick_forward",
    )(info, y1, y2, gain, segments, weight)


def backward(info, y1, c1, c2, gain, segments, dg, saved, weight):
    rows = y1.shape[0]
    return pl.pallas_call(
        backward_kernel,
        out_shape=(
            shape((rows, D)), shape((rows, 4 * D)), shape((rows, D)),
            shape((rows, D)), shape((1, D), f32),
        ),
        in_specs=[smem()] + [vmem()] * 10 + [anyspace()],
        out_specs=(vmem(),) * 5,
        scratch_shapes=[
            pltpu.VMEM((D, 4 * D), bf16), pltpu.VMEM((rows, D), f32),
            pltpu.SemaphoreType.DMA((CHUNKS,)),
        ],
        cost_estimate=pl.CostEstimate(
            flops=8 * rows * D * D, bytes_accessed=12 * MIB, transcendentals=rows * FF
        ),
        name="tick_backward",
    )(info, y1, c1, c2, gain, segments, dg, *saved, weight)


def grad_kernel(place, dtype, info_ref, *refs):
    count = 2 * TICKS
    lefts, rights, out_ref, turned_ref = refs[:count], refs[count:2 * count], refs[-2], refs[-1]
    rows = lefts[0].shape[0]

    @pl.when(pl.program_id(0) == 0)
    def _():
        for index, left in enumerate(lefts):
            for half in range(2):
                block = left[:, cols(2 * half + place, QUARTER)]
                turned_ref[half, :, cols(index, rows)] = block.T

    split = jnp.where(info_ref[0] == 0, 3 * D // CHUNK, FF // CHUNK)
    half = jnp.where(pl.program_id(0) >= split, 1, 0)
    turned = turned_ref[half]
    right = jnp.concatenate([ref[...] for ref in rights], axis=0)
    out_ref[...] = dot(turned, right).astype(dtype)


def grad_block(info, lefts, rights, place, dtype):
    rows = lefts[0].shape[0]
    count = len(lefts)

    def body(*refs):
        grad_kernel(place, dtype, *refs)

    return pl.pallas_call(
        body,
        out_shape=shape((QUARTER, 4 * D), dtype),
        grid=(CHUNKS,),
        in_specs=[smem()]
        + [pl.BlockSpec((rows, D), lambda j: (0, 0))] * count
        + [pl.BlockSpec((rows, CHUNK), lambda j: (0, j))] * count,
        out_specs=pl.BlockSpec((QUARTER, CHUNK), lambda j: (0, j)),
        scratch_shapes=[pltpu.VMEM((2, QUARTER, count * rows), bf16)],
        cost_estimate=pl.CostEstimate(
            flops=2 * count * rows * D * D, bytes_accessed=10 * MIB, transcendentals=0
        ),
        name="grad_own" if place == 0 else "grad_other",
    )(info, *lefts, *rights)


def shards(streams, cotangents, weights, norm_gains, segment_ids):
    section = lax.axis_index("section")
    replica = lax.axis_index("dp")
    sections = lax.axis_size("section")
    replicas = lax.axis_size("dp")
    weight = weights[0]
    rows = streams.shape[3]
    segments = segment_ids[:, 0]
    ring = [(s, (s - 1) % sections) for s in range(sections)]

    def pass_on(value):
        return lax.ppermute(value, "section", ring)

    def exchange(value, bits):
        return lax.ppermute(value, "dp", [(r, r ^ bits) for r in range(replicas)])

    y1, y2 = streams[0, 0, 0], streams[1, 0, 0]
    c1, c2 = cotangents[0, 0, 0], cotangents[1, 0, 0]
    dg = jnp.zeros((1, D), f32)
    lefts, rights = [], []
    for tick in range(TICKS):
        anchor = (section + tick) % sections
        info = jnp.stack([section % 2, anchor, replica // 2, replica % 2]).astype(jnp.int32)
        next_y2 = pass_on(y1)
        next_c1 = pass_on(c2)
        a, *saved = forward(info, y1, y2, norm_gains, segments, weight)
        next_y1 = pass_on(a)
        c, right, keep, send, dg = backward(
            info, y1, c1, c2, norm_gains, segments, dg, saved, weight
        )
        next_c2 = pass_on(c)
        lefts += [keep, exchange(send, 1)]
        rights += [right, exchange(right, 1)]
        y1, y2, c1, c2 = next_y1, next_y2, next_c1, next_c2
    dg_all = dg + exchange(dg, 1) + exchange(dg, 2) + exchange(dg, 3)
    grad_other = grad_block(info, lefts, rights, 1, bf16)
    received = exchange(grad_other, 2)
    grad_own = grad_block(info, lefts, rights, 0, f32)
    grad_scale = 1.0 / math.sqrt(TICKS * rows * replicas)
    weight_grads = ((grad_own + received.astype(f32)) * grad_scale).astype(bf16)[None]
    gain_grads = lax.dynamic_slice_in_dim(dg_all, replica * QUARTER, QUARTER, 1) * grad_scale
    out_streams = jnp.stack([y1, y2])[:, None, None]
    out_cotangents = jnp.stack([c1, c2])[:, None, None]
    return (out_streams, out_cotangents, weight_grads, gain_grads)


def solution(mesh):
    placed = (
        P(None, "section", "dp", None, None),
        P(None, "section", "dp", None, None),
        P("section", None, None),
        P("section", None),
        P(None, "dp", None),
    )
    return jax.shard_map(
        shards,
        mesh=mesh,
        in_specs=placed,
        out_specs=(
            P(None, "section", "dp", None, None),
            P(None, "section", "dp", None, None),
            P("section", "dp", None),
            P("section", "dp"),
        ),
        check_vma=False,
    )
```

```python
from functools import partial
import math

import jax
import jax.numpy as jnp
from jax import lax
from jax.experimental import pallas as pl
from jax.experimental.pallas import tpu as pltpu
from jax.sharding import PartitionSpec as P


D = 1024
FF = 2048
TICKS = 3
CHUNK = 512
CHUNKS = 4 * D // CHUNK
PAIR = 128
QUARTER = D // 4

epsilon = 1e-05
bf16 = jnp.bfloat16
f32 = jnp.float32

NN = (((1,), (0,)), ((), ()))
NT = (((1,), (1,)), ((), ()))
TN = (((0,), (0,)), ((), ()))


def dot(first, second, dims=NN):
    return lax.dot_general(first, second, dims, preferred_element_type=f32)


def cols(index, width):
    return pl.ds(index * width, width)


def weight_copies(w_hbm, w_ref, sems, order):
    copies = {}
    for chunk in order:
        piece = cols(chunk, CHUNK)
        copies[chunk] = pltpu.make_async_copy(
            w_hbm.at[:, piece], w_ref.at[:, piece], sems.at[chunk]
        )
    for chunk in order:
        copies[chunk].start()
    return copies


def low_lanes(rows):
    return lax.broadcasted_iota(jnp.int32, (rows, PAIR), 1) < 64


def half_sums(values, low):
    first = jnp.sum(jnp.where(low, values, 0.0), axis=-1, keepdims=True)
    second = jnp.sum(jnp.where(low, 0.0, values), axis=-1, keepdims=True)
    return first, second


def attention_mask(anchor, seg_ref):
    rows = seg_ref.shape[1]
    segment = seg_ref[pl.ds(anchor, 1), :].astype(f32)
    across = jnp.broadcast_to(segment, (rows, rows))
    down = across.T
    row_index = lax.broadcasted_iota(jnp.int32, (rows, rows), 0)
    col_index = lax.broadcasted_iota(jnp.int32, (rows, rows), 1)
    allowed = (across == down) & (col_index <= row_index)
    mask = jnp.where(allowed, 1.0, 0.0)
    return jnp.concatenate([mask, mask], axis=0)


def split_pair(values, low_b, high_b):
    return jnp.concatenate([values * low_b, values * high_b], axis=0)


def pair_weights(q_ref, k_ref, lane, mask, low_b, high_b):
    q_split = split_pair(q_ref[:, lane], low_b, high_b)
    k = k_ref[:, lane]
    scores = dot(q_split, k, NT) * 0.125
    raised = jnp.exp(scores) * mask
    total = jnp.sum(raised, axis=-1, keepdims=True)
    return q_split, k, raised / total


GELU_A = math.sqrt(2.0 / math.pi)
GELU_B = 0.044715


class Ready:
    def wait(self):
        pass


RESIDENT = (Ready(),) * CHUNKS


def first_forward_kernel(tick, info_ref, y1_ref, y2_ref, g_ref, seg_ref, w_hbm,
                         a_ref, n_ref, x2_ref, s1_ref, s2_ref, w_ref, acc_ref, sems):
    copies = weight_copies(w_hbm, w_ref, sems, range(CHUNKS))
    forward_body(copies, tick, info_ref, y1_ref, y2_ref, g_ref, seg_ref, w_ref,
                 a_ref, n_ref, x2_ref, s1_ref, s2_ref, acc_ref)


def forward_kernel(tick, *refs):
    forward_body(RESIDENT, tick, *refs)


def forward_body(copies, tick, info_ref, y1_ref, y2_ref, g_ref, seg_ref, w_ref,
                 a_ref, n_ref, x2_ref, s1_ref, s2_ref, acc_ref):
    rows = y1_ref.shape[0]
    stream = y1_ref[...].astype(f32)
    mean_square = jnp.mean(stream * stream, axis=-1, keepdims=True)
    n_ref[...] = (stream * lax.rsqrt(mean_square + epsilon) * g_ref[...]).astype(bf16)

    @pl.when(info_ref[0] == 0)
    def _():
        low = low_lanes(rows)
        low_b = jnp.where(low, 1.0, 0.0).astype(bf16)
        high_b = jnp.where(low, 0.0, 1.0).astype(bf16)
        lane_index = lax.broadcasted_iota(jnp.int32, (rows, PAIR), 1)
        scales = jnp.zeros((rows, PAIR), f32)
        for chunk in range(6):
            copies[chunk].wait()
            projected = dot(n_ref[...], w_ref[:, cols(chunk, CHUNK)])
            for inner in range(CHUNK // PAIR):
                part = projected[:, inner * PAIR:(inner + 1) * PAIR]
                pair = chunk * (CHUNK // PAIR) + inner
                if chunk < 4:
                    first, second = half_sums(part * part, low)
                    r_first = lax.rsqrt(first * (1.0 / 64) + epsilon)
                    r_second = lax.rsqrt(second * (1.0 / 64) + epsilon)
                    scales = jnp.where(lane_index == 2 * pair, r_first, scales)
                    scales = jnp.where(lane_index == 2 * pair + 1, r_second, scales)
                    part = part * jnp.where(low, r_first, r_second)
                s2_ref[:, cols(pair, PAIR)] = part.astype(bf16)
        s1_ref[:, :PAIR] = scales
        mask = attention_mask(info_ref[3 + tick], seg_ref)
        for pair in range(8):
            _, _, weights = pair_weights(
                s2_ref.at[:, :D], s2_ref.at[:, D:2 * D], cols(pair, PAIR), mask, low_b, high_b
            )
            soft = weights.astype(bf16)
            v = s2_ref[:, cols(16 + pair, PAIR)]
            mixed = dot(soft[:rows], v * low_b) + dot(soft[rows:], v * high_b)
            x2_ref[:, cols(pair, PAIR)] = mixed.astype(bf16)
        for chunk in (6, 7):
            copies[chunk].wait()
            out = cols(chunk - 6, CHUNK)
            branch = dot(x2_ref[:, :D], w_ref[:, cols(chunk, CHUNK)])
            a_ref[:, out] = (y2_ref[:, out].astype(f32) - branch).astype(bf16)

    @pl.when(info_ref[0] == 1)
    def _():
        for chunk in range(4):
            copies[chunk].wait()
            piece = cols(chunk, CHUNK)
            pre = dot(n_ref[...], w_ref[:, piece])
            square = pre * pre
            bend = jnp.tanh(GELU_A * (pre + GELU_B * (pre * square)))
            half = 0.5 * (1.0 + bend)
            x2_ref[:, piece] = (pre * half).astype(bf16)
            slope = GELU_A * (1.0 + (3.0 * GELU_B) * square)
            s1_ref[:, piece] = half + 0.5 * pre * (1.0 - bend * bend) * slope
        for chunk in range(4, 8):
            copies[chunk].wait()
            term = dot(x2_ref[:, cols(chunk - 4, CHUNK)], w_ref[:, cols(chunk, CHUNK)], NT)
            if chunk == 4:
                acc_ref[...] = term
            else:
                acc_ref[...] += term
        a_ref[...] = (y2_ref[...].astype(f32) - acc_ref[...]).astype(bf16)


def first_backward_kernel(tick, *refs):
    backward_kernel(tick, *refs[:6], None, *refs[6:])


def backward_kernel(tick, info_ref, y1_ref, c1_ref, c2_ref, g_ref, seg_ref, dg_in_ref,
                    n_ref, x2_ref, s1_ref, s2_ref, w_ref,
                    c_ref, right_ref, keep_ref, send_ref, dg_ref, acc_ref):
    copies = RESIDENT
    rows = y1_ref.shape[0]
    chip, core = info_ref[1], info_ref[2]
    blocks = (2 * chip + core, 2 * (1 - chip) + core)
    other = (2 * chip + 1 - core, 2 * (1 - chip) + 1 - core)

    def spread(left, half):
        for place, (mine, theirs) in enumerate(zip(blocks, other)):
            out = cols(2 * half + place, QUARTER)
            keep_ref[:, out] = left[:, pl.ds(pl.multiple_of(mine * QUARTER, QUARTER), QUARTER)]
            send_ref[:, out] = left[:, pl.ds(pl.multiple_of(theirs * QUARTER, QUARTER), QUARTER)]

    spread(n_ref, 0)

    @pl.when(info_ref[0] == 0)
    def _():
        spread(x2_ref, 1)
        right_ref[:, 3 * D:] = c2_ref[...]
        low = low_lanes(rows)
        low_b = jnp.where(low, 1.0, 0.0).astype(bf16)
        high_b = jnp.where(low, 0.0, 1.0).astype(bf16)
        mask = attention_mask(info_ref[3 + tick], seg_ref)
        for chunk in (6, 7):
            copies[chunk].wait()
            term = dot(c2_ref[:, cols(chunk - 6, CHUNK)], w_ref[:, cols(chunk, CHUNK)], NT)
            if chunk == 6:
                acc_ref[...] = term
            else:
                acc_ref[...] += term

        def norm_back(dy, y_b, pair):
            dy = dy.astype(bf16).astype(f32)
            y = y_b.astype(f32)
            first, second = half_sums(dy * y, low)
            mean = jnp.where(low, first, second) * (1.0 / 64)
            scale = jnp.where(low, s1_ref[:, 2 * pair:2 * pair + 1], s1_ref[:, 2 * pair + 1:2 * pair + 2])
            return (scale * (dy - y * mean)).astype(bf16)

        for pair in range(8):
            lane = cols(pair, PAIR)
            q_split, k, weights = pair_weights(
                s2_ref.at[:, :D], s2_ref.at[:, D:2 * D], lane, mask, low_b, high_b
            )
            soft = weights.astype(bf16)
            v = s2_ref[:, cols(16 + pair, PAIR)]
            d_mix = split_pair(acc_ref[:, lane].astype(bf16), low_b, high_b)
            d_soft = dot(d_mix, v, NT).astype(bf16).astype(f32)
            dv = dot(soft, d_mix, TN)
            product = d_soft * weights
            d_scores = (product - weights * jnp.sum(product, axis=-1, keepdims=True)) * 0.125
            d_scores = d_scores.astype(bf16)
            dq = dot(d_scores[:rows], k * low_b) + dot(d_scores[rows:], k * high_b)
            dk = dot(d_scores, q_split, TN)
            right_ref[:, lane] = norm_back(dq, s2_ref[:, lane], pair)
            right_ref[:, cols(8 + pair, PAIR)] = norm_back(dk, k, 8 + pair)
            right_ref[:, cols(16 + pair, PAIR)] = dv.astype(bf16)
        for chunk in (4, 5, 0, 1, 2, 3):
            copies[chunk].wait()
            term = dot(right_ref[:, cols(chunk, CHUNK)], w_ref[:, cols(chunk, CHUNK)], NT)
            if chunk == 4:
                acc_ref[...] = term
            else:
                acc_ref[...] += term

    @pl.when(info_ref[0] == 1)
    def _():
        spread(c2_ref, 1)
        right_ref[:, FF:] = x2_ref[...]
        for chunk in (6, 7, 4, 5):
            copies[chunk].wait()
            piece = cols(chunk - 4, CHUNK)
            grad = dot(c2_ref[...], w_ref[:, cols(chunk, CHUNK)])
            right_ref[:, piece] = (grad * s1_ref[:, piece]).astype(bf16)
        for chunk in range(4):
            copies[chunk].wait()
            term = dot(right_ref[:, cols(chunk, CHUNK)], w_ref[:, cols(chunk, CHUNK)], NT)
            if chunk == 0:
                acc_ref[...] = term
            else:
                acc_ref[...] += term

    stream = y1_ref[...].astype(f32)
    inverse = lax.rsqrt(jnp.mean(stream * stream, axis=-1, keepdims=True) + epsilon)
    unit = stream * inverse
    grad_normed = acc_ref[...]
    dg = jnp.sum(grad_normed * unit, axis=0, keepdims=True)
    dg_ref[...] = dg if dg_in_ref is None else dg_in_ref[...] + dg
    scaled = grad_normed * g_ref[...]
    du = inverse * (scaled - unit * jnp.mean(scaled * unit, axis=-1, keepdims=True))
    c_ref[...] = (c1_ref[...].astype(f32) + du).astype(bf16)


def vmem():
    return pl.BlockSpec(memory_space=pltpu.VMEM)


def smem():
    return pl.BlockSpec(memory_space=pltpu.SMEM)


def hbm():
    return pl.BlockSpec(memory_space=pltpu.HBM)


def held(value):
    return pltpu.with_memory_space_constraint(value, pltpu.VMEM)


def shape(dims, dtype=bf16):
    return jax.ShapeDtypeStruct(dims, dtype)


MIB = 1 << 20


def forward(tick, info, y1, y2, gain, segments, weight):
    rows = y1.shape[0]
    first = tick == 0
    fixed = pltpu.with_memory_space_constraint(weight, pltpu.HBM) if first else None
    saved = (
        pltpu.VMEM((rows, D), bf16), pltpu.VMEM((rows, FF), bf16),
        pltpu.VMEM((rows, FF), f32), pltpu.VMEM((rows, 3 * D), bf16),
    )
    scratch = [pltpu.VMEM((rows, D), f32)]
    resident = ()
    if first:
        resident = (pltpu.VMEM((D, 4 * D), bf16),)
        scratch.append(pltpu.SemaphoreType.DMA((CHUNKS,)))
    return pl.pallas_call(
        partial(first_forward_kernel if first else forward_kernel, tick),
        out_shape=(shape((rows, D)),) + saved + resident,
        in_specs=[smem()] + [vmem()] * 4 + [hbm() if first else vmem()],
        out_specs=(vmem(),) * (5 + len(resident)),
        scratch_shapes=scratch,
        compiler_params=pltpu.CompilerParams(vmem_limit_bytes=16 * MIB),
        cost_estimate=pl.CostEstimate(
            flops=8 * rows * D * D, bytes_accessed=12 * MIB, transcendentals=rows * FF
        ),
        name="tick_forward",
    )(info, y1, y2, gain, segments, fixed if first else held(weight))


def backward(tick, info, y1, c1, c2, gain, segments, dg, saved, weight):
    rows = y1.shape[0]
    carried = [] if tick == 0 else [dg]
    return pl.pallas_call(
        partial(first_backward_kernel if tick == 0 else backward_kernel, tick),
        out_shape=(
            shape((rows, D)), shape((rows, 4 * D)), shape((rows, D)),
            shape((rows, D)), shape((1, D), f32),
        ),
        in_specs=[smem()] + [vmem()] * (10 + len(carried)),
        out_specs=(vmem(),) * 5,
        scratch_shapes=[pltpu.VMEM((rows, D), f32)],
        compiler_params=pltpu.CompilerParams(vmem_limit_bytes=16 * MIB),
        cost_estimate=pl.CostEstimate(
            flops=8 * rows * D * D, bytes_accessed=12 * MIB, transcendentals=rows * FF
        ),
        name="tick_backward",
    )(info, y1, c1, c2, gain, segments, *carried, *saved, held(weight))


def grad_kernel(place, info_ref, *refs):
    count = 2 * TICKS
    lefts, rights, out_ref, turned_ref = refs[:count], refs[count:2 * count], refs[-2], refs[-1]
    rows = lefts[0].shape[0]
    for index, left in enumerate(lefts):
        for half in range(2):
            block = left[:, cols(2 * half + place, QUARTER)]
            turned_ref[half, :, cols(index, rows)] = block.T
    split = jnp.where(info_ref[0] == 0, 3 * D // CHUNK, FF // CHUNK)

    def step(chunk, carry):
        half = jnp.where(chunk >= split, 1, 0)
        piece = pl.ds(pl.multiple_of(chunk * CHUNK, CHUNK), CHUNK)
        right = jnp.concatenate([ref[:, piece] for ref in rights], axis=0)
        out_ref[:, piece] = dot(turned_ref[half], right).astype(out_ref.dtype)
        return carry

    lax.fori_loop(0, CHUNKS, step, 0)


def grad_block(info, lefts, rights, place, dtype):
    rows = lefts[0].shape[0]
    count = len(lefts)
    return pl.pallas_call(
        partial(grad_kernel, place),
        out_shape=shape((QUARTER, 4 * D), dtype),
        in_specs=[smem()] + [vmem()] * (2 * count),
        out_specs=vmem(),
        scratch_shapes=[pltpu.VMEM((2, QUARTER, count * rows), bf16)],
        compiler_params=pltpu.CompilerParams(vmem_limit_bytes=20 * MIB),
        cost_estimate=pl.CostEstimate(
            flops=2 * count * rows * D * D, bytes_accessed=10 * MIB, transcendentals=0
        ),
        name="grad_own" if place == 0 else "grad_other",
    )(info, *map(held, lefts), *map(held, rights))


def shards(streams, cotangents, weights, norm_gains, segment_ids):
    section = lax.axis_index("section")
    replica = lax.axis_index("dp")
    sections = lax.axis_size("section")
    replicas = lax.axis_size("dp")
    weight = weights[0]
    rows = streams.shape[3]
    segments = segment_ids[:, 0]
    ring = [(s, (s - 1) % sections) for s in range(sections)]

    def pass_on(value):
        return lax.ppermute(value, "section", ring)

    def exchange(value, bits):
        return lax.ppermute(value, "dp", [(r, r ^ bits) for r in range(replicas)])

    y1, y2 = streams[0, 0, 0], streams[1, 0, 0]
    c1, c2 = cotangents[0, 0, 0], cotangents[1, 0, 0]
    anchors = [(section + tick) % sections for tick in range(TICKS)]
    info = jnp.stack([section % 2, replica // 2, replica % 2] + anchors).astype(jnp.int32)
    dg = None
    lefts, rights = [], []
    for tick in range(TICKS):
        next_y2 = pass_on(y1)
        next_c1 = pass_on(c2)
        a, *saved = forward(tick, info, y1, y2, norm_gains, segments, weight)
        if tick == 0:
            weight = saved.pop()
        next_y1 = pass_on(a)
        c, right, keep, send, dg = backward(
            tick, info, y1, c1, c2, norm_gains, segments, dg, saved, weight
        )
        next_c2 = pass_on(c)
        lefts += [keep, exchange(send, 1)]
        rights += [right, exchange(right, 1)]
        y1, y2, c1, c2 = next_y1, next_y2, next_c1, next_c2
    dg_all = dg + exchange(dg, 1) + exchange(dg, 2) + exchange(dg, 3)
    grad_other = grad_block(info, lefts, rights, 1, bf16)
    received = exchange(grad_other, 2)
    grad_own = grad_block(info, lefts, rights, 0, f32)
    grad_scale = 1.0 / math.sqrt(TICKS * rows * replicas)
    weight_grads = ((grad_own + received.astype(f32)) * grad_scale).astype(bf16)[None]
    gain_grads = lax.dynamic_slice_in_dim(dg_all, replica * QUARTER, QUARTER, 1) * grad_scale
    out_streams = jnp.stack([y1, y2])[:, None, None]
    out_cotangents = jnp.stack([c1, c2])[:, None, None]
    return (out_streams, out_cotangents, weight_grads, gain_grads)


def solution(mesh):
    placed = (
        P(None, "section", "dp", None, None),
        P(None, "section", "dp", None, None),
        P("section", None, None),
        P("section", None),
        P(None, "dp", None),
    )
    return jax.shard_map(
        shards,
        mesh=mesh,
        in_specs=placed,
        out_specs=(
            P(None, "section", "dp", None, None),
            P(None, "section", "dp", None, None),
            P("section", "dp", None),
            P("section", "dp"),
        ),
        check_vma=False,
    )
```

```python
from functools import partial
import math

import jax
import jax.numpy as jnp
from jax import lax
from jax.experimental import pallas as pl
from jax.experimental.pallas import tpu as pltpu
from jax.sharding import PartitionSpec as P


D = 1024
FF = 2048
TICKS = 3
CHUNK = 512
CHUNKS = 4 * D // CHUNK
PAIR = 128
UNROLL = 2
RELAYS = {"p2": 1, "a": 2, "c": 3}
QUARTER = D // 4

epsilon = 1e-05
bf16 = jnp.bfloat16
f32 = jnp.float32

NN = (((1,), (0,)), ((), ()))
NT = (((1,), (1,)), ((), ()))
TN = (((0,), (0,)), ((), ()))


def dot(first, second, dims=NN):
    return lax.dot_general(first, second, dims, preferred_element_type=f32)


def cols(index, width):
    start = index * width
    return pl.ds(start if isinstance(start, int) else pl.multiple_of(start, width), width)


def add_terms(acc_ref, rows_ref, w_ref, count, offset):
    acc_ref[...] = dot(rows_ref[:, cols(0, CHUNK)], w_ref[:, cols(offset, CHUNK)], NT)

    def step(chunk, carry):
        acc_ref[...] += dot(rows_ref[:, cols(chunk, CHUNK)], w_ref[:, cols(chunk + offset, CHUNK)], NT)
        return carry

    lax.fori_loop(1, count, step, 0)


def weight_copies(w_hbm, w_ref, sems, order):
    copies = {}
    for chunk in order:
        piece = cols(chunk, CHUNK)
        copies[chunk] = pltpu.make_async_copy(
            w_hbm.at[:, piece], w_ref.at[:, piece], sems.at[chunk]
        )
    for chunk in order:
        copies[chunk].start()
    return copies


def low_lanes(rows):
    return lax.broadcasted_iota(jnp.int32, (rows, PAIR), 1) < 64


def half_sums(values, low):
    first = jnp.sum(jnp.where(low, values, 0.0), axis=-1, keepdims=True)
    second = jnp.sum(jnp.where(low, 0.0, values), axis=-1, keepdims=True)
    return first, second


def attention_mask(anchor, seg_ref):
    rows = seg_ref.shape[1]
    segment = seg_ref[pl.ds(anchor, 1), :].astype(f32)
    across = jnp.broadcast_to(segment, (rows, rows))
    down = across.T
    row_index = lax.broadcasted_iota(jnp.int32, (rows, rows), 0)
    col_index = lax.broadcasted_iota(jnp.int32, (rows, rows), 1)
    allowed = (across == down) & (col_index <= row_index)
    mask = jnp.where(allowed, 1.0, 0.0)
    return jnp.concatenate([mask, mask], axis=0)


def split_pair(values, low_b, high_b):
    return jnp.concatenate([values * low_b, values * high_b], axis=0)


def pair_weights(q_ref, k_ref, lane, mask, low_b, high_b):
    q_split = split_pair(q_ref[:, lane], low_b, high_b)
    k = k_ref[:, lane]
    scores = dot(q_split, k, NT) * 0.125
    raised = jnp.exp(scores) * mask
    total = jnp.sum(raised, axis=-1, keepdims=True)
    return q_split, k, raised / total


GELU_A = math.sqrt(2.0 / math.pi)
GELU_B = 0.044715


class Ready:
    def wait(self):
        pass


RESIDENT = (Ready(),) * CHUNKS


def first_forward_kernel(tick, info_ref, y1_ref, y2_ref, g_ref, seg_ref, w_hbm,
                         a_ref, n_ref, x2_ref, s1_ref, s2_ref, w_ref, acc_ref, sems):
    copies = weight_copies(w_hbm, w_ref, sems, range(CHUNKS))
    forward_body(copies, tick, info_ref, y1_ref, y2_ref, g_ref, seg_ref, w_ref,
                 a_ref, n_ref, x2_ref, s1_ref, s2_ref, acc_ref)


def forward_kernel(tick, *refs):
    forward_body(RESIDENT, tick, *refs)


def forward_body(copies, tick, info_ref, y1_ref, y2_ref, g_ref, seg_ref, w_ref,
                 a_ref, n_ref, x2_ref, s1_ref, s2_ref, acc_ref):
    rows = y1_ref.shape[0]
    stream = y1_ref[...].astype(f32)
    mean_square = jnp.mean(stream * stream, axis=-1, keepdims=True)
    n_ref[...] = (stream * lax.rsqrt(mean_square + epsilon) * g_ref[...]).astype(bf16)

    @pl.when(info_ref[0] == 0)
    def _():
        low = low_lanes(rows)
        low_b = jnp.where(low, 1.0, 0.0).astype(bf16)
        high_b = jnp.where(low, 0.0, 1.0).astype(bf16)
        for chunk in range(6):
            copies[chunk].wait()
            projected = dot(n_ref[...], w_ref[:, cols(chunk, CHUNK)])
            for inner in range(CHUNK // PAIR):
                part = projected[:, inner * PAIR:(inner + 1) * PAIR]
                pair = chunk * (CHUNK // PAIR) + inner
                if chunk < 4:
                    first, second = half_sums(part * part, low)
                    r_first = lax.rsqrt(first * (1.0 / 64) + epsilon)
                    r_second = lax.rsqrt(second * (1.0 / 64) + epsilon)
                    scale = jnp.where(low, r_first, r_second)
                    s1_ref[:, cols(pair, PAIR)] = scale
                    part = part * scale
                s2_ref[:, cols(pair, PAIR)] = part.astype(bf16)
        mask = attention_mask(info_ref[3 + tick], seg_ref)
        for pair in range(8):
            _, _, weights = pair_weights(
                s2_ref.at[:, :D], s2_ref.at[:, D:2 * D], cols(pair, PAIR), mask, low_b, high_b
            )
            soft = weights.astype(bf16)
            v = s2_ref[:, cols(16 + pair, PAIR)]
            mixed = dot(soft[:rows], v * low_b) + dot(soft[rows:], v * high_b)
            x2_ref[:, cols(pair, PAIR)] = mixed.astype(bf16)
        for chunk in (6, 7):
            copies[chunk].wait()
            out = cols(chunk - 6, CHUNK)
            branch = dot(x2_ref[:, :D], w_ref[:, cols(chunk, CHUNK)])
            a_ref[:, out] = (y2_ref[:, out].astype(f32) - branch).astype(bf16)

    @pl.when(info_ref[0] == 1)
    def _():
        def hidden_step(chunk, carry):
            piece = cols(chunk, CHUNK)
            pre = dot(n_ref[...], w_ref[:, piece])
            square = pre * pre
            bend = jnp.tanh(GELU_A * (pre + GELU_B * (pre * square)))
            half = 0.5 * (1.0 + bend)
            x2_ref[:, piece] = (pre * half).astype(bf16)
            slope = GELU_A * (1.0 + (3.0 * GELU_B) * square)
            s1_ref[:, piece] = half + 0.5 * pre * (1.0 - bend * bend) * slope
            return carry

        if copies is RESIDENT:
            lax.fori_loop(0, 4, hidden_step, 0)
            add_terms(acc_ref, x2_ref, w_ref, 4, 4)
        else:
            for chunk in range(4):
                copies[chunk].wait()
                hidden_step(chunk, 0)
            for chunk in range(4, 8):
                copies[chunk].wait()
            add_terms(acc_ref, x2_ref, w_ref, 4, 4)
        a_ref[...] = (y2_ref[...].astype(f32) - acc_ref[...]).astype(bf16)


def first_backward_kernel(tick, *refs):
    backward_kernel(tick, *refs[:6], None, *refs[6:])


def backward_kernel(tick, info_ref, y1_ref, c1_ref, c2_ref, g_ref, seg_ref, dg_in_ref,
                    n_ref, x2_ref, s1_ref, s2_ref, w_ref,
                    c_ref, right_ref, keep_ref, send_ref, dg_ref, acc_ref):
    rows = y1_ref.shape[0]
    chip, core = info_ref[1], info_ref[2]
    blocks = (2 * chip + core, 2 * (1 - chip) + core)
    other = (2 * chip + 1 - core, 2 * (1 - chip) + 1 - core)

    def spread(left, half):
        for place, (mine, theirs) in enumerate(zip(blocks, other)):
            out = cols(2 * half + place, QUARTER)
            keep_ref[:, out] = left[:, pl.ds(pl.multiple_of(mine * QUARTER, QUARTER), QUARTER)]
            send_ref[:, out] = left[:, pl.ds(pl.multiple_of(theirs * QUARTER, QUARTER), QUARTER)]

    spread(n_ref, 0)

    @pl.when(info_ref[0] == 0)
    def _():
        spread(x2_ref, 1)
        right_ref[:, 3 * D:] = c2_ref[...]
        low = low_lanes(rows)
        low_b = jnp.where(low, 1.0, 0.0).astype(bf16)
        high_b = jnp.where(low, 0.0, 1.0).astype(bf16)
        mask = attention_mask(info_ref[3 + tick], seg_ref)
        add_terms(acc_ref, c2_ref, w_ref, 2, 6)

        def norm_back(dy, y_b, pair):
            dy = dy.astype(bf16).astype(f32)
            y = y_b.astype(f32)
            first, second = half_sums(dy * y, low)
            mean = jnp.where(low, first, second) * (1.0 / 64)
            return (s1_ref[:, cols(pair, PAIR)] * (dy - y * mean)).astype(bf16)

        def pair_back(pair):
            lane = cols(pair, PAIR)
            q_split, k, weights = pair_weights(
                s2_ref.at[:, :D], s2_ref.at[:, D:2 * D], lane, mask, low_b, high_b
            )
            soft = weights.astype(bf16)
            v = s2_ref[:, cols(16 + pair, PAIR)]
            d_mix = split_pair(acc_ref[:, lane].astype(bf16), low_b, high_b)
            d_soft = dot(d_mix, v, NT).astype(bf16).astype(f32)
            dv = dot(soft, d_mix, TN)
            product = d_soft * weights
            d_scores = (product - weights * jnp.sum(product, axis=-1, keepdims=True)) * 0.125
            d_scores = d_scores.astype(bf16)
            dq = dot(d_scores[:rows], k * low_b) + dot(d_scores[rows:], k * high_b)
            dk = dot(d_scores, q_split, TN)
            right_ref[:, lane] = norm_back(dq, s2_ref[:, lane], pair)
            right_ref[:, cols(8 + pair, PAIR)] = norm_back(dk, k, 8 + pair)
            right_ref[:, cols(16 + pair, PAIR)] = dv.astype(bf16)

        def pair_step(step, carry):
            for inner in range(UNROLL):
                pair_back(step * UNROLL + inner)
            return carry

        lax.fori_loop(0, 8 // UNROLL, pair_step, 0)
        add_terms(acc_ref, right_ref, w_ref, 6, 0)

    @pl.when(info_ref[0] == 1)
    def _():
        spread(c2_ref, 1)
        right_ref[:, FF:] = x2_ref[...]

        def hidden_step(chunk, carry):
            piece = cols(chunk, CHUNK)
            grad = dot(c2_ref[...], w_ref[:, cols(chunk + 4, CHUNK)])
            right_ref[:, piece] = (grad * s1_ref[:, piece]).astype(bf16)
            return carry

        lax.fori_loop(0, 4, hidden_step, 0)
        add_terms(acc_ref, right_ref, w_ref, 4, 0)

    stream = y1_ref[...].astype(f32)
    inverse = lax.rsqrt(jnp.mean(stream * stream, axis=-1, keepdims=True) + epsilon)
    unit = stream * inverse
    grad_normed = acc_ref[...]
    dg = jnp.sum(grad_normed * unit, axis=0, keepdims=True)
    dg_ref[...] = dg if dg_in_ref is None else dg_in_ref[...] + dg
    scaled = grad_normed * g_ref[...]
    du = inverse * (scaled - unit * jnp.mean(scaled * unit, axis=-1, keepdims=True))
    c_ref[...] = (c1_ref[...].astype(f32) + du).astype(bf16)


def vmem():
    return pl.BlockSpec(memory_space=pltpu.VMEM)


def smem():
    return pl.BlockSpec(memory_space=pltpu.SMEM)


def hbm():
    return pl.BlockSpec(memory_space=pltpu.HBM)


def held(value):
    return pltpu.with_memory_space_constraint(value, pltpu.VMEM)


def shape(dims, dtype=bf16):
    return jax.ShapeDtypeStruct(dims, dtype)


MIB = 1 << 20


def forward(tick, info, y1, y2, gain, segments, weight):
    rows = y1.shape[0]
    first = tick == 0
    fixed = pltpu.with_memory_space_constraint(weight, pltpu.HBM) if first else None
    saved = (
        pltpu.VMEM((rows, D), bf16), pltpu.VMEM((rows, FF), bf16),
        pltpu.VMEM((rows, FF), f32), pltpu.VMEM((rows, 3 * D), bf16),
    )
    scratch = [pltpu.VMEM((rows, D), f32)]
    resident = ()
    if first:
        resident = (pltpu.VMEM((D, 4 * D), bf16),)
        scratch.append(pltpu.SemaphoreType.DMA((CHUNKS,)))
    return pl.pallas_call(
        partial(first_forward_kernel if first else forward_kernel, tick),
        out_shape=(shape((rows, D)),) + saved + resident,
        in_specs=[smem()] + [vmem()] * 4 + [hbm() if first else vmem()],
        out_specs=(vmem(),) * (5 + len(resident)),
        scratch_shapes=scratch,
        compiler_params=pltpu.CompilerParams(vmem_limit_bytes=16 * MIB),
        cost_estimate=pl.CostEstimate(
            flops=8 * rows * D * D, bytes_accessed=12 * MIB, transcendentals=rows * FF
        ),
        name="tick_forward",
    )(info, y1, y2, gain, segments, fixed if first else held(weight))


def backward(tick, info, y1, c1, c2, gain, segments, dg, saved, weight):
    rows = y1.shape[0]
    carried = [] if tick == 0 else [dg]
    return pl.pallas_call(
        partial(first_backward_kernel if tick == 0 else backward_kernel, tick),
        out_shape=(
            shape((rows, D)), shape((rows, 4 * D)), shape((rows, D)),
            shape((rows, D)), shape((1, D), f32),
        ),
        in_specs=[smem()] + [vmem()] * (10 + len(carried)),
        out_specs=(vmem(),) * 5,
        scratch_shapes=[pltpu.VMEM((rows, D), f32)],
        compiler_params=pltpu.CompilerParams(vmem_limit_bytes=16 * MIB),
        cost_estimate=pl.CostEstimate(
            flops=8 * rows * D * D, bytes_accessed=12 * MIB, transcendentals=rows * FF
        ),
        name="tick_backward",
    )(info, y1, c1, c2, gain, segments, *carried, *saved, held(weight))


def grad_kernel(place, info_ref, *refs):
    count = 2 * TICKS
    lefts, rights, out_ref, turned_ref = refs[:count], refs[count:2 * count], refs[-2], refs[-1]
    rows = lefts[0].shape[0]
    for index, left in enumerate(lefts):
        for half in range(2):
            block = left[:, cols(2 * half + place, QUARTER)]
            turned_ref[half, :, cols(index, rows)] = block.T
    split = jnp.where(info_ref[0] == 0, 3 * D // CHUNK, FF // CHUNK)

    def step(chunk, carry):
        half = jnp.where(chunk >= split, 1, 0)
        piece = pl.ds(pl.multiple_of(chunk * CHUNK, CHUNK), CHUNK)
        right = jnp.concatenate([ref[:, piece] for ref in rights], axis=0)
        out_ref[:, piece] = dot(turned_ref[half], right).astype(out_ref.dtype)
        return carry

    lax.fori_loop(0, CHUNKS, step, 0)


def grad_block(info, lefts, rights, place, dtype):
    rows = lefts[0].shape[0]
    count = len(lefts)
    return pl.pallas_call(
        partial(grad_kernel, place),
        out_shape=shape((QUARTER, 4 * D), dtype),
        in_specs=[smem()] + [vmem()] * (2 * count),
        out_specs=vmem(),
        scratch_shapes=[pltpu.VMEM((2, QUARTER, count * rows), bf16)],
        compiler_params=pltpu.CompilerParams(vmem_limit_bytes=20 * MIB),
        cost_estimate=pl.CostEstimate(
            flops=2 * count * rows * D * D, bytes_accessed=10 * MIB, transcendentals=0
        ),
        name="grad_own" if place == 0 else "grad_other",
    )(info, *map(held, lefts), *map(held, rights))


def shards(streams, cotangents, weights, norm_gains, segment_ids):
    section = lax.axis_index("section")
    replica = lax.axis_index("dp")
    sections = lax.axis_size("section")
    replicas = lax.axis_size("dp")
    weight = weights[0]
    rows = streams.shape[3]
    segments = segment_ids[:, 0]
    ring = [(s, (s - 1) % sections) for s in range(sections)]

    def pass_on(value):
        return lax.ppermute(value, "section", ring)

    half = sections // 2

    def pass_relayed(value, column):
        direct = [(s, s - 1) for s in range(sections) if s % half]
        up = [(0, half + column), (half, column)]
        down = [(half + column, sections - 1), (column, half - 1)]
        lifted = lax.ppermute(value, "section", up)
        near = lax.ppermute(value, "section", direct)
        far = lax.ppermute(lifted, "section", down)
        return jnp.where(section % half == half - 1, far, near)

    def send(name, value, tick):
        if tick == TICKS - 1 and name in RELAYS:
            return pass_relayed(value, RELAYS[name] * half // 4)
        return pass_on(value)

    def exchange(value, bits):
        return lax.ppermute(value, "dp", [(r, r ^ bits) for r in range(replicas)])

    y1, y2 = streams[0, 0, 0], streams[1, 0, 0]
    c1, c2 = cotangents[0, 0, 0], cotangents[1, 0, 0]
    anchors = [(section + tick) % sections for tick in range(TICKS)]
    info = jnp.stack([section % 2, replica // 2, replica % 2] + anchors).astype(jnp.int32)
    dg = None
    lefts, rights = [], []
    for tick in range(TICKS):
        next_y2 = send("p1", y1, tick)
        next_c1 = send("p2", c2, tick)
        a, *saved = forward(tick, info, y1, y2, norm_gains, segments, weight)
        if tick == 0:
            weight = saved.pop()
        next_y1 = send("a", a, tick)
        c, right, keep, give, dg = backward(
            tick, info, y1, c1, c2, norm_gains, segments, dg, saved, weight
        )
        next_c2 = send("c", c, tick)
        lefts += [keep, exchange(give, 1)]
        rights += [right, exchange(right, 1)]
        y1, y2, c1, c2 = next_y1, next_y2, next_c1, next_c2
    dg_all = dg + exchange(dg, 1) + exchange(dg, 2) + exchange(dg, 3)
    grad_other = grad_block(info, lefts, rights, 1, bf16)
    received = exchange(grad_other, 2)
    grad_own = grad_block(info, lefts, rights, 0, f32)
    grad_scale = 1.0 / math.sqrt(TICKS * rows * replicas)
    weight_grads = ((grad_own + received.astype(f32)) * grad_scale).astype(bf16)[None]
    gain_grads = lax.dynamic_slice_in_dim(dg_all, replica * QUARTER, QUARTER, 1) * grad_scale
    out_streams = jnp.stack([y1, y2])[:, None, None]
    out_cotangents = jnp.stack([c1, c2])[:, None, None]
    return (out_streams, out_cotangents, weight_grads, gain_grads)


def solution(mesh):
    placed = (
        P(None, "section", "dp", None, None),
        P(None, "section", "dp", None, None),
        P("section", None, None),
        P("section", None),
        P(None, "dp", None),
    )
    return jax.shard_map(
        shards,
        mesh=mesh,
        in_specs=placed,
        out_specs=(
            P(None, "section", "dp", None, None),
            P(None, "section", "dp", None, None),
            P("section", "dp", None),
            P("section", "dp"),
        ),
        check_vma=False,
    )
```

```python
from functools import partial
import math

import jax
import jax.numpy as jnp
from jax import lax
from jax.experimental import pallas as pl
from jax.experimental.pallas import tpu as pltpu
from jax.sharding import PartitionSpec as P


D = 1024
FF = 2048
TICKS = 3
CHUNK = 512
CHUNKS = 4 * D // CHUNK
PAIR = 128
UNROLL = 2
RELAYS = {"p2": 1, "a": 2, "c": 3}
QUARTER = D // 4

epsilon = 1e-05
bf16 = jnp.bfloat16
f32 = jnp.float32

NN = (((1,), (0,)), ((), ()))
NT = (((1,), (1,)), ((), ()))
TN = (((0,), (0,)), ((), ()))


def dot(first, second, dims=NN):
    return lax.dot_general(first, second, dims, preferred_element_type=f32)


def cols(index, width):
    start = index * width
    return pl.ds(start if isinstance(start, int) else pl.multiple_of(start, width), width)


def add_terms(acc_ref, rows_ref, w_ref, count, offset):
    acc_ref[...] = dot(rows_ref[:, cols(0, CHUNK)], w_ref[:, cols(offset, CHUNK)], NT)

    def step(chunk, carry):
        acc_ref[...] += dot(rows_ref[:, cols(chunk, CHUNK)], w_ref[:, cols(chunk + offset, CHUNK)], NT)
        return carry

    lax.fori_loop(1, count, step, 0)


def weight_copies(w_hbm, w_ref, sems, order):
    copies = {}
    for chunk in order:
        piece = cols(chunk, CHUNK)
        copies[chunk] = pltpu.make_async_copy(
            w_hbm.at[:, piece], w_ref.at[:, piece], sems.at[chunk]
        )
    for chunk in order:
        copies[chunk].start()
    return copies


def low_lanes(rows):
    return lax.broadcasted_iota(jnp.int32, (rows, PAIR), 1) < 64


def half_sums(values, low):
    first = jnp.sum(jnp.where(low, values, 0.0), axis=-1, keepdims=True)
    second = jnp.sum(jnp.where(low, 0.0, values), axis=-1, keepdims=True)
    return first, second


def attention_mask(anchor, seg_ref):
    rows = seg_ref.shape[1]
    segment = seg_ref[pl.ds(anchor, 1), :].astype(f32)
    across = jnp.broadcast_to(segment, (rows, rows))
    down = across.T
    row_index = lax.broadcasted_iota(jnp.int32, (rows, rows), 0)
    col_index = lax.broadcasted_iota(jnp.int32, (rows, rows), 1)
    allowed = (across == down) & (col_index <= row_index)
    mask = jnp.where(allowed, 1.0, 0.0)
    return jnp.concatenate([mask, mask], axis=0)


def split_pair(values, low_b, high_b):
    return jnp.concatenate([values * low_b, values * high_b], axis=0)


def pair_weights(q_ref, k_ref, lane, mask, low_b, high_b):
    q_split = split_pair(q_ref[:, lane], low_b, high_b)
    k = k_ref[:, lane]
    scores = dot(q_split, k, NT) * 0.125
    raised = jnp.exp(scores) * mask
    total = jnp.sum(raised, axis=-1, keepdims=True)
    return q_split, k, raised / total


GELU_A = math.sqrt(2.0 / math.pi)
GELU_B = 0.044715


class Ready:
    def wait(self):
        pass


RESIDENT = (Ready(),) * CHUNKS


def first_forward_kernel(tick, info_ref, y1_ref, y2_ref, g_ref, seg_ref, w_hbm,
                         a_ref, n_ref, x2_ref, s1_ref, s2_ref, w_ref, acc_ref, sems):
    copies = weight_copies(w_hbm, w_ref, sems, range(CHUNKS))
    forward_body(copies, tick, info_ref, y1_ref, y2_ref, g_ref, seg_ref, w_ref,
                 a_ref, n_ref, x2_ref, s1_ref, s2_ref, acc_ref)


def forward_kernel(tick, *refs):
    forward_body(RESIDENT, tick, *refs)


def last_forward_kernel(tick, *refs):
    forward_body(RESIDENT, tick, *refs[:2], None, *refs[2:])


def last_backward_kernel(tick, *refs):
    backward_kernel(tick, *refs[:2], None, *refs[2:])


def forward_body(copies, tick, info_ref, y1_ref, y2_ref, g_ref, seg_ref, w_ref,
                 a_ref, n_ref, x2_ref, s1_ref, s2_ref, acc_ref):
    rows = y1_ref.shape[0]
    stream = y1_ref[...].astype(f32)
    mean_square = jnp.mean(stream * stream, axis=-1, keepdims=True)
    n_ref[...] = (stream * lax.rsqrt(mean_square + epsilon) * g_ref[...]).astype(bf16)

    @pl.when(info_ref[0] == 0)
    def _():
        low = low_lanes(rows)
        low_b = jnp.where(low, 1.0, 0.0).astype(bf16)
        high_b = jnp.where(low, 0.0, 1.0).astype(bf16)
        for chunk in range(6):
            copies[chunk].wait()
            projected = dot(n_ref[...], w_ref[:, cols(chunk, CHUNK)])
            for inner in range(CHUNK // PAIR):
                part = projected[:, inner * PAIR:(inner + 1) * PAIR]
                pair = chunk * (CHUNK // PAIR) + inner
                if chunk < 4:
                    first, second = half_sums(part * part, low)
                    r_first = lax.rsqrt(first * (1.0 / 64) + epsilon)
                    r_second = lax.rsqrt(second * (1.0 / 64) + epsilon)
                    scale = jnp.where(low, r_first, r_second)
                    s1_ref[:, cols(pair, PAIR)] = scale
                    part = part * scale
                s2_ref[:, cols(pair, PAIR)] = part.astype(bf16)
        mask = attention_mask(info_ref[3 + tick], seg_ref)
        for pair in range(8):
            _, _, weights = pair_weights(
                s2_ref.at[:, :D], s2_ref.at[:, D:2 * D], cols(pair, PAIR), mask, low_b, high_b
            )
            soft = weights.astype(bf16)
            v = s2_ref[:, cols(16 + pair, PAIR)]
            mixed = dot(soft[:rows], v * low_b) + dot(soft[rows:], v * high_b)
            x2_ref[:, cols(pair, PAIR)] = mixed.astype(bf16)
        for chunk in (6, 7):
            copies[chunk].wait()
            out = cols(chunk - 6, CHUNK)
            branch = dot(x2_ref[:, :D], w_ref[:, cols(chunk, CHUNK)])
            if y2_ref is None:
                a_ref[:, out] = branch
            else:
                a_ref[:, out] = (y2_ref[:, out].astype(f32) - branch).astype(bf16)

    @pl.when(info_ref[0] == 1)
    def _():
        def hidden_step(chunk, carry):
            piece = cols(chunk, CHUNK)
            pre = dot(n_ref[...], w_ref[:, piece])
            square = pre * pre
            bend = jnp.tanh(GELU_A * (pre + GELU_B * (pre * square)))
            half = 0.5 * (1.0 + bend)
            x2_ref[:, piece] = (pre * half).astype(bf16)
            slope = GELU_A * (1.0 + (3.0 * GELU_B) * square)
            s1_ref[:, piece] = half + 0.5 * pre * (1.0 - bend * bend) * slope
            return carry

        if copies is RESIDENT:
            lax.fori_loop(0, 4, hidden_step, 0)
            add_terms(acc_ref, x2_ref, w_ref, 4, 4)
        else:
            for chunk in range(4):
                copies[chunk].wait()
                hidden_step(chunk, 0)
            for chunk in range(4, 8):
                copies[chunk].wait()
            add_terms(acc_ref, x2_ref, w_ref, 4, 4)
        if y2_ref is None:
            a_ref[...] = acc_ref[...]
        else:
            a_ref[...] = (y2_ref[...].astype(f32) - acc_ref[...]).astype(bf16)


def first_backward_kernel(tick, *refs):
    backward_kernel(tick, *refs[:6], None, *refs[6:])


def backward_kernel(tick, info_ref, y1_ref, c1_ref, c2_ref, g_ref, seg_ref, dg_in_ref,
                    n_ref, x2_ref, s1_ref, s2_ref, w_ref,
                    c_ref, right_ref, keep_ref, send_ref, dg_ref, acc_ref):
    rows = y1_ref.shape[0]
    chip, core = info_ref[1], info_ref[2]
    blocks = (2 * chip + core, 2 * (1 - chip) + core)
    other = (2 * chip + 1 - core, 2 * (1 - chip) + 1 - core)

    def spread(left, half):
        for place, (mine, theirs) in enumerate(zip(blocks, other)):
            out = cols(2 * half + place, QUARTER)
            keep_ref[:, out] = left[:, pl.ds(pl.multiple_of(mine * QUARTER, QUARTER), QUARTER)]
            send_ref[:, out] = left[:, pl.ds(pl.multiple_of(theirs * QUARTER, QUARTER), QUARTER)]

    spread(n_ref, 0)

    @pl.when(info_ref[0] == 0)
    def _():
        spread(x2_ref, 1)
        right_ref[:, 3 * D:] = c2_ref[...]
        low = low_lanes(rows)
        low_b = jnp.where(low, 1.0, 0.0).astype(bf16)
        high_b = jnp.where(low, 0.0, 1.0).astype(bf16)
        mask = attention_mask(info_ref[3 + tick], seg_ref)
        add_terms(acc_ref, c2_ref, w_ref, 2, 6)

        def norm_back(dy, y_b, pair):
            dy = dy.astype(bf16).astype(f32)
            y = y_b.astype(f32)
            first, second = half_sums(dy * y, low)
            mean = jnp.where(low, first, second) * (1.0 / 64)
            return (s1_ref[:, cols(pair, PAIR)] * (dy - y * mean)).astype(bf16)

        def pair_back(pair):
            lane = cols(pair, PAIR)
            q_split, k, weights = pair_weights(
                s2_ref.at[:, :D], s2_ref.at[:, D:2 * D], lane, mask, low_b, high_b
            )
            soft = weights.astype(bf16)
            v = s2_ref[:, cols(16 + pair, PAIR)]
            d_mix = split_pair(acc_ref[:, lane].astype(bf16), low_b, high_b)
            d_soft = dot(d_mix, v, NT).astype(bf16).astype(f32)
            dv = dot(soft, d_mix, TN)
            product = d_soft * weights
            d_scores = (product - weights * jnp.sum(product, axis=-1, keepdims=True)) * 0.125
            d_scores = d_scores.astype(bf16)
            dq = dot(d_scores[:rows], k * low_b) + dot(d_scores[rows:], k * high_b)
            dk = dot(d_scores, q_split, TN)
            right_ref[:, lane] = norm_back(dq, s2_ref[:, lane], pair)
            right_ref[:, cols(8 + pair, PAIR)] = norm_back(dk, k, 8 + pair)
            right_ref[:, cols(16 + pair, PAIR)] = dv.astype(bf16)

        def pair_step(step, carry):
            for inner in range(UNROLL):
                pair_back(step * UNROLL + inner)
            return carry

        lax.fori_loop(0, 8 // UNROLL, pair_step, 0)
        add_terms(acc_ref, right_ref, w_ref, 6, 0)

    @pl.when(info_ref[0] == 1)
    def _():
        spread(c2_ref, 1)
        right_ref[:, FF:] = x2_ref[...]

        def hidden_step(chunk, carry):
            piece = cols(chunk, CHUNK)
            grad = dot(c2_ref[...], w_ref[:, cols(chunk + 4, CHUNK)])
            right_ref[:, piece] = (grad * s1_ref[:, piece]).astype(bf16)
            return carry

        lax.fori_loop(0, 4, hidden_step, 0)
        add_terms(acc_ref, right_ref, w_ref, 4, 0)

    stream = y1_ref[...].astype(f32)
    inverse = lax.rsqrt(jnp.mean(stream * stream, axis=-1, keepdims=True) + epsilon)
    unit = stream * inverse
    grad_normed = acc_ref[...]
    dg = jnp.sum(grad_normed * unit, axis=0, keepdims=True)
    dg_ref[...] = dg if dg_in_ref is None else dg_in_ref[...] + dg
    scaled = grad_normed * g_ref[...]
    du = inverse * (scaled - unit * jnp.mean(scaled * unit, axis=-1, keepdims=True))
    c_ref[...] = du if c1_ref is None else (c1_ref[...].astype(f32) + du).astype(bf16)


def vmem():
    return pl.BlockSpec(memory_space=pltpu.VMEM)


def smem():
    return pl.BlockSpec(memory_space=pltpu.SMEM)


def hbm():
    return pl.BlockSpec(memory_space=pltpu.HBM)


def held(value):
    return pltpu.with_memory_space_constraint(value, pltpu.VMEM)


def shape(dims, dtype=bf16):
    return jax.ShapeDtypeStruct(dims, dtype)


MIB = 1 << 20


def forward(tick, info, y1, y2, gain, segments, weight):
    rows = y1.shape[0]
    first, last = tick == 0, tick == TICKS - 1
    ends = [] if last else [held(y2)]
    kernel = first_forward_kernel if first else last_forward_kernel if last else forward_kernel
    fixed = pltpu.with_memory_space_constraint(weight, pltpu.HBM) if first else None
    saved = (
        pltpu.VMEM((rows, D), bf16), pltpu.VMEM((rows, FF), bf16),
        pltpu.VMEM((rows, FF), f32), pltpu.VMEM((rows, 3 * D), bf16),
    )
    scratch = [pltpu.VMEM((rows, D), f32)]
    resident = ()
    if first:
        resident = (pltpu.VMEM((D, 4 * D), bf16),)
        scratch.append(pltpu.SemaphoreType.DMA((CHUNKS,)))
    return pl.pallas_call(
        partial(kernel, tick),
        out_shape=(shape((rows, D), f32 if last else bf16),) + saved + resident,
        in_specs=[smem()] + [vmem()] * (3 + len(ends)) + [hbm() if first else vmem()],
        out_specs=(vmem(),) * (5 + len(resident)),
        scratch_shapes=scratch,
        compiler_params=pltpu.CompilerParams(vmem_limit_bytes=16 * MIB),
        cost_estimate=pl.CostEstimate(
            flops=8 * rows * D * D, bytes_accessed=12 * MIB, transcendentals=rows * FF
        ),
        name="tick_forward",
    )(info, held(y1), *ends, gain, segments, fixed if first else held(weight))


def backward(tick, info, y1, c1, c2, gain, segments, dg, saved, weight):
    rows = y1.shape[0]
    first, last = tick == 0, tick == TICKS - 1
    carried = [] if first else [dg]
    ends = [] if last else [held(c1)]
    kernel = first_backward_kernel if first else last_backward_kernel if last else backward_kernel
    return pl.pallas_call(
        partial(kernel, tick),
        out_shape=(
            shape((rows, D), f32 if last else bf16), shape((rows, 4 * D)), shape((rows, D)),
            shape((rows, D)), shape((1, D), f32),
        ),
        in_specs=[smem()] + [vmem()] * (9 + len(carried) + len(ends)),
        out_specs=(vmem(),) * 5,
        scratch_shapes=[pltpu.VMEM((rows, D), f32)],
        compiler_params=pltpu.CompilerParams(vmem_limit_bytes=16 * MIB),
        cost_estimate=pl.CostEstimate(
            flops=8 * rows * D * D, bytes_accessed=12 * MIB, transcendentals=rows * FF
        ),
        name="tick_backward",
    )(info, held(y1), *ends, held(c2), gain, segments, *carried, *saved, held(weight))


def grad_kernel(place, start, info_ref, *refs):
    count = 2 * TICKS
    lefts, rights, out_ref, turned_ref = refs[:count], refs[count:2 * count], refs[-2], refs[-1]
    rows = lefts[0].shape[0]
    for index, left in enumerate(lefts):
        for half in range(2):
            block = left[:, cols(2 * half + place, QUARTER)]
            turned_ref[half, :, cols(index, rows)] = block.T
    split = jnp.where(info_ref[0] == 0, 3 * D // CHUNK, FF // CHUNK)

    def step(chunk, carry):
        half = jnp.where(chunk >= split, 1, 0)
        right = jnp.concatenate([ref[:, cols(chunk, CHUNK)] for ref in rights], axis=0)
        out_ref[:, cols(chunk - start, CHUNK)] = dot(turned_ref[half], right).astype(out_ref.dtype)
        return carry

    lax.fori_loop(start, start + out_ref.shape[1] // CHUNK, step, 0)


def grad_block(info, lefts, rights, place, dtype, start, width):
    rows = lefts[0].shape[0]
    count = len(lefts)
    return pl.pallas_call(
        partial(grad_kernel, place, start),
        out_shape=pltpu.VMEM((QUARTER, width * CHUNK), dtype),
        in_specs=[smem()] + [vmem()] * (2 * count),
        out_specs=vmem(),
        scratch_shapes=[pltpu.VMEM((2, QUARTER, count * rows), bf16)],
        compiler_params=pltpu.CompilerParams(vmem_limit_bytes=20 * MIB),
        cost_estimate=pl.CostEstimate(
            flops=width * count * rows * D * D // 4, bytes_accessed=width * MIB, transcendentals=0
        ),
        name="grad_own" if place == 0 else "grad_other",
    )(info, *map(held, lefts), *map(held, rights))


def finish(own, received, so_far, start, scale):
    width = received.shape[1] // CHUNK

    def body(own_ref, received_ref, *refs):
        step = pl.program_id(0)
        total = own_ref[:, cols(step + start, CHUNK)] + received_ref[:, cols(step, CHUNK)].astype(f32)
        refs[-1][...] = (total * scale).astype(bf16)

    before = [] if so_far is None else [so_far]
    return pl.pallas_call(
        body,
        out_shape=shape(own.shape),
        grid=(width,),
        in_specs=[vmem(), vmem()] + [hbm()] * len(before),
        out_specs=pl.BlockSpec((QUARTER, CHUNK), lambda j: (0, j + start)),
        input_output_aliases={2: 0} if before else {},
        compiler_params=pltpu.CompilerParams(vmem_limit_bytes=16 * MIB),
        cost_estimate=pl.CostEstimate(
            flops=width * MIB, bytes_accessed=width * MIB, transcendentals=0
        ),
        name="finish",
    )(held(own), held(received), *before)


def shards(streams, cotangents, weights, norm_gains, segment_ids):
    section = lax.axis_index("section")
    replica = lax.axis_index("dp")
    sections = lax.axis_size("section")
    replicas = lax.axis_size("dp")
    weight = weights[0]
    rows = streams.shape[3]
    segments = segment_ids[:, 0]
    ring = [(s, (s - 1) % sections) for s in range(sections)]

    def pass_on(value):
        return lax.ppermute(value, "section", ring)

    half = sections // 2

    def pass_relayed(value, column):
        direct = [(s, s - 1) for s in range(sections) if s % half]
        up = [(0, half + column), (half, column)]
        down = [(half + column, sections - 1), (column, half - 1)]
        lifted = lax.ppermute(value, "section", up)
        near = lax.ppermute(value, "section", direct)
        far = lax.ppermute(lifted, "section", down)
        return jnp.where(section % half == half - 1, far, near)

    def send(name, value, tick):
        if tick == TICKS - 1 and name in RELAYS:
            return pass_relayed(value, RELAYS[name] * half // 4 - 1)
        return pass_on(value)

    def exchange(value, bits):
        return lax.ppermute(value, "dp", [(r, r ^ bits) for r in range(replicas)])

    y1, y2 = streams[0, 0, 0], streams[1, 0, 0]
    c1, c2 = cotangents[0, 0, 0], cotangents[1, 0, 0]
    anchors = [(section + tick) % sections for tick in range(TICKS)]
    info = jnp.stack([section % 2, replica // 2, replica % 2] + anchors).astype(jnp.int32)
    dg = None
    lefts, rights = [], []
    for tick in range(TICKS):
        next_y2 = send("p1", y1, tick)
        next_c1 = send("p2", c2, tick)
        a, *saved = forward(tick, info, y1, y2, norm_gains, segments, weight)
        if tick == 0:
            weight = saved.pop()
        if tick == TICKS - 1:
            a = (y2.astype(f32) - a).astype(bf16)
        next_y1 = send("a", a, tick)
        c, right, keep, give, dg = backward(
            tick, info, y1, c1, c2, norm_gains, segments, dg, saved, weight
        )
        if tick == TICKS - 1:
            c = (c1.astype(f32) + c).astype(bf16)
        next_c2 = send("c", c, tick)
        lefts += [keep, exchange(give, 1)]
        rights += [right, exchange(right, 1)]
        y1, y2, c1, c2 = next_y1, next_y2, next_c1, next_c2
    dg_all = dg + exchange(dg, 1) + exchange(dg, 2) + exchange(dg, 3)
    half_width = CHUNKS // 2
    received = []
    for part in range(2):
        grad_other = grad_block(
            info, lefts, rights, 1, bf16, part * half_width, half_width
        )
        received.append(exchange(grad_other, 2))
    grad_own = grad_block(info, lefts, rights, 0, f32, 0, CHUNKS)
    grad_scale = 1.0 / math.sqrt(TICKS * rows * replicas)
    weight_grads = None
    for part in range(2):
        weight_grads = finish(grad_own, received[part], weight_grads, part * half_width, grad_scale)
    weight_grads = weight_grads[None]
    gain_grads = lax.dynamic_slice_in_dim(dg_all, replica * QUARTER, QUARTER, 1) * grad_scale
    out_streams = jnp.stack([y1, y2])[:, None, None]
    out_cotangents = jnp.stack([c1, c2])[:, None, None]
    return (out_streams, out_cotangents, weight_grads, gain_grads)


def solution(mesh):
    placed = (
        P(None, "section", "dp", None, None),
        P(None, "section", "dp", None, None),
        P("section", None, None),
        P("section", None),
        P(None, "dp", None),
    )
    return jax.shard_map(
        shards,
        mesh=mesh,
        in_specs=placed,
        out_specs=(
            P(None, "section", "dp", None, None),
            P(None, "section", "dp", None, None),
            P("section", "dp", None),
            P("section", "dp"),
        ),
        check_vma=False,
    )
```
